32 devices in a mesh: fsdp: 8 (over z, core), tp: 4 (over y, x).
Axes of the slice: x: 2, y: 2, z: 4, core: 2. Of those that a mesh axis runs over, the one named last changes fastest.
Arguments:
- grad: bfloat16 [3, 5120, 27648], P(None, 'fsdp', 'tp'), may hold values from -50 to 50
- momentum: bfloat16 [3, 5120, 27648], P(None, 'fsdp', 'tp'), may hold values from -50 to 50
- basis: bfloat16 [27648, 3, 256], P(('tp', 'fsdp')), may hold values from -0.0390625 to 0.0390625
Outputs:
- momentum_next: bfloat16 [3, 5120, 27648], P(None, 'fsdp', 'tp')
- basis_next: bfloat16 [27648, 3, 256], P(('tp', 'fsdp'))
- update: bfloat16 [3, 5120, 27648], P(None, 'fsdp', 'tp')
The draws below stay inside these ranges and needn't reach their ends.
All inputs are finite; a program needn't handle non-finite values.
Results may differ from the reference program's by a relative error of at most 0.0078.
Values may be sent and summed in bfloat16 or wider, within the bound.
A program may use at most 192 MiB of HBM per device.

```python
import math
import jax
import jax.numpy as jnp
from jax import lax

D = 5120
FF = 27648
RANK = 256
LAYER_COUNT = 3


def scaled_field(key):
    first, second, third = jax.random.split(key, 3)
    position = jnp.arange(FF, dtype=jnp.float32).reshape(1, 1, FF) / (FF - 1)
    base = jnp.clip(jax.random.normal(first, (LAYER_COUNT, D, FF), jnp.float32), -5.0, 5.0)
    row_scale = jnp.exp(jax.random.uniform(second, (LAYER_COUNT, D, 1), jnp.float32, -0.8, 0.8))
    col_scale = jnp.exp(jax.random.uniform(third, (LAYER_COUNT, 1, FF), jnp.float32, -0.8, 0.8))
    ramp = 1.0 + position
    return base * row_scale * col_scale * ramp


def draw_grad(key, part):
    return scaled_field(jax.random.fold_in(key, 11)).astype(jnp.bfloat16)


def draw_momentum(key, part):
    return scaled_field(jax.random.fold_in(key, 23)).astype(jnp.bfloat16)


def draw_basis(key, part):
    first, second = jax.random.split(jax.random.fold_in(key, 37))
    common = jnp.clip(jax.random.normal(first, (FF, LAYER_COUNT, 1), jnp.float32), -3.5, 3.5)
    single = jnp.clip(jax.random.normal(second, (FF, LAYER_COUNT, RANK), jnp.float32), -3.5, 3.5)
    mixed = 0.70710677 * common + 0.70710677 * single
    return (mixed / 128.0).astype(jnp.bfloat16)


def setup_inputs(seed: int = 0) -> dict:
    key_list = jax.random.split(jax.random.key(seed), 4)
    return {
        "grad": draw_grad(jax.random.fold_in(key_list[3], 71), 0),
        "momentum": draw_momentum(jax.random.fold_in(key_list[3], 71), 0),
        "basis": draw_basis(jax.random.fold_in(key_list[3], 71), 0),
    }


MOMENTUM_DECAY = 0.8
EPSILON = 1e-06

def reference(grad, momentum, basis):
    scale = math.sqrt(D * FF / RANK)
    hi = lax.Precision.HIGHEST
    moms = []
    bases = []
    updates = []
    for layer in range(LAYER_COUNT):
        buffer = MOMENTUM_DECAY * momentum[layer].astype(jnp.float32) + grad[layer].astype(jnp.float32)
        momentum_buffer16 = buffer.astype(jnp.bfloat16)
        power_output = jnp.dot(momentum_buffer16.astype(jnp.float32), basis[:, layer, :].astype(jnp.float32), preferred_element_type=jnp.float32)
        gram = jnp.dot(power_output.T, power_output, precision=hi)
        lower = jnp.linalg.cholesky(gram)
        inverse_matrix = jax.scipy.linalg.solve_triangular(lower, jnp.eye(RANK, dtype=jnp.float32), lower=True)
        ortho = jnp.dot(power_output, inverse_matrix.T, precision=hi).astype(jnp.bfloat16)
        project = jnp.dot(momentum_buffer16.T.astype(jnp.float32), ortho.astype(jnp.float32), preferred_element_type=jnp.float32)
        colsq = lax.optimization_barrier(jnp.sum(project * project, axis=0))
        basis_next = (project * lax.rsqrt(colsq + EPSILON)).astype(jnp.bfloat16)
        project16 = project.astype(jnp.bfloat16)
        feedback = jnp.dot(ortho.astype(jnp.float32), project16.T.astype(jnp.float32), preferred_element_type=jnp.float32)
        moms.append((buffer - (1.0 - MOMENTUM_DECAY) * feedback).astype(jnp.bfloat16))
        bases.append(basis_next)
        updates.append((scale * jnp.dot(ortho.astype(jnp.float32), basis_next.T.astype(jnp.float32), preferred_element_type=jnp.float32)).astype(jnp.bfloat16))
    return (jnp.stack(moms), jnp.stack(bases, axis=1), jnp.stack(updates))
```

```python
import math

import jax
import jax.numpy as jnp
from jax import lax
from jax.experimental import pallas as pl
from jax.experimental.pallas import tpu as pltpu
from jax.sharding import PartitionSpec as P

MOMENTUM_DECAY = 0.8
EPSILON = 1e-06
HIGHEST = lax.Precision.HIGHEST
TILE = 8
BLOCK = 64


def inverse_kernel(gram_ref, out_ref, work_ref):
    layers, rank, _ = gram_ref.shape
    wide = 2 * BLOCK
    lane = lax.broadcasted_iota(jnp.int32, (BLOCK, wide), 1)
    row = lax.broadcasted_iota(jnp.int32, (BLOCK, wide), 0)
    eye = jnp.where(lane - BLOCK == row, 1.0, 0.0).astype(jnp.float32)
    sub = lax.broadcasted_iota(jnp.int32, (TILE, wide), 0)
    whole_row = lax.broadcasted_iota(jnp.int32, (rank, rank), 0)
    whole_col = lax.broadcasted_iota(jnp.int32, (rank, rank), 1)
    for l in range(layers):
        work_ref[l, :, :rank] = gram_ref[l]
        work_ref[l, :, rank:] = jnp.where(whole_row == whole_col, 1.0, 0.0).astype(jnp.float32)
    count = BLOCK // TILE
    for first in range(0, rank, BLOCK):
        tiles = []
        for l in range(layers):
            aligned = first // wide * wide
            square = work_ref[l, first : first + BLOCK, aligned : aligned + wide]
            if first != aligned:
                square = pltpu.roll(square, BLOCK, 1)
            square = jnp.where(lane < BLOCK, square, eye)
            tiles.append([square[t * TILE : (t + 1) * TILE] for t in range(count)])
        for k in range(BLOCK):
            own, inner = divmod(k, TILE)
            for l in range(layers):
                pivot = tiles[l][own][inner : inner + 1, k : k + 1]
                scale = lax.rsqrt(pivot)
                scale = scale * (1.5 - 0.5 * pivot * scale * scale)
                line = tiles[l][own][inner : inner + 1, :] * scale
                for t in range(own, count):
                    tile = tiles[l][t]
                    new = tile - (tile[:, k : k + 1] * scale) * line
                    if t == own:
                        new = jnp.where(sub > inner, new, jnp.where(sub == inner, line, tile))
                    tiles[l][t] = new
        for l in range(layers):
            factor = pltpu.roll(jnp.concatenate(tiles[l], axis=0), BLOCK, 1)[:, :BLOCK]
            rows = jnp.dot(
                factor,
                work_ref[l, first : first + BLOCK, :],
                precision=HIGHEST,
                preferred_element_type=jnp.float32,
            )
            out_ref[l, first : first + BLOCK, :] = rows[:, rank:]
            below = first + BLOCK
            if below < rank:
                change = lax.dot_general(
                    rows[:, :rank],
                    rows,
                    (((0,), (0,)), ((), ())),
                    precision=HIGHEST,
                    preferred_element_type=jnp.float32,
                )
                work_ref[l, below:, :] = work_ref[l, below:, :] - change[below:, :]


def inverse_factor(gram):
    layers, rank, _ = gram.shape
    return pl.pallas_call(
        inverse_kernel,
        out_shape=jax.ShapeDtypeStruct(gram.shape, jnp.float32),
        in_specs=[pl.BlockSpec(memory_space=pltpu.VMEM)],
        out_specs=pl.BlockSpec(memory_space=pltpu.VMEM),
        scratch_shapes=[pltpu.VMEM((layers, rank, 2 * rank), jnp.float32)],
        name="inverse_factor",
    )(gram)


def pairwise_sum(value, axis, size):
    if size & (size - 1):
        return lax.psum(value, axis)
    step = 1
    while step < size:
        value = value + lax.ppermute(value, axis, [(i, i ^ step) for i in range(size)])
        step *= 2
    return value


def build(mesh):
    fsdp, tp = mesh.shape["fsdp"], mesh.shape["tp"]

    def shards(grad, momentum, basis):
        layers, rank = basis.shape[1:]
        rows, columns = grad.shape[1] * fsdp, grad.shape[2] * tp
        hi_scale = math.sqrt(rows * columns / rank)
        full = [lax.all_gather(basis[:, l], "fsdp", axis=0, tiled=True) for l in range(layers)]

        buffer = MOMENTUM_DECAY * momentum.astype(jnp.float32) + grad.astype(jnp.float32)
        block = lax.optimization_barrier(buffer.astype(jnp.bfloat16))

        partial = jnp.stack(
            [jnp.dot(block[l], full[l], preferred_element_type=jnp.float32) for l in range(layers)]
        )
        power = lax.psum(partial, "tp")
        gram = lax.psum(
            jnp.einsum("lmr,lms->lrs", power, power, precision=HIGHEST), "fsdp"
        )
        inverse = inverse_factor(gram)
        ortho = jnp.einsum("lmz,liz->lmi", power, inverse, precision=HIGHEST).astype(jnp.bfloat16)

        shares = []
        for l in range(layers):
            term = lax.dot_general(
                block[l], ortho[l], (((0,), (0,)), ((), ())), preferred_element_type=jnp.float32
            ).astype(jnp.bfloat16)
            shares.append(lax.psum_scatter(term, "fsdp", scatter_dimension=0, tiled=True))
        gathered = [lax.all_gather(share, "fsdp", axis=0, tiled=True) for share in shares]

        project = [share.astype(jnp.float32) for share in shares]
        colsq = jnp.stack([jnp.sum(p * p, axis=0) for p in project])
        colsq = pairwise_sum(pairwise_sum(colsq, "fsdp", fsdp), "tp", tp)
        norm = lax.rsqrt(colsq + EPSILON)
        basis_next = jnp.stack(
            [(project[l] * norm[l]).astype(jnp.bfloat16) for l in range(layers)], axis=1
        )
        scaled = (ortho.astype(jnp.float32) * (hi_scale * norm)[:, None, :]).astype(jnp.bfloat16)

        project16 = jnp.stack(gathered)
        feedback = jnp.einsum("lmr,lnr->lmn", ortho, project16, preferred_element_type=jnp.float32)
        momentum_next = (buffer - (1.0 - MOMENTUM_DECAY) * feedback).astype(jnp.bfloat16)
        direction = jnp.einsum("lmr,lnr->lmn", scaled, project16, preferred_element_type=jnp.float32)
        return momentum_next, basis_next, direction.astype(jnp.bfloat16)

    return shards


def solution(mesh):
    matrix, factor = P(None, "fsdp", "tp"), P(("tp", "fsdp"), None, None)
    return jax.shard_map(
        build(mesh),
        mesh=mesh,
        in_specs=(matrix, matrix, factor),
        out_specs=(matrix, factor, matrix),
        check_vma=False,
    )
```
